32 devices in a mesh: expert: 16 (over z, y, x), dp: 2 (over core).
Axes of the slice: x: 2, y: 2, z: 4, core: 2. Of those that a mesh axis runs over, the one named last changes fastest.
Arguments:
- tokens: bfloat16 [2, 256, 4096], P(None, ('expert', 'dp')), may hold values from -6 to 6
- norm_gain: float32 [4096], replicated, may hold values from 0.5 to 1.5
- route_ids: int32 [2, 256, 8], P(None, ('expert', 'dp')), may hold values from 0 to 15, all different within a row; in each aligned block of 8 rows (0 to 7, 8 to 15, ..., all dimensions but the last counted through in order) at most 8 rows name the same one
- route_weights: float32 [2, 256, 8], P(None, ('expert', 'dp')), may hold values from 0.05 to 0.25
- rows_left: int32 [256], P(('expert', 'dp')), may hold values from 1 to 40
- gate_up_elems: bfloat16 [16, 2, 4096, 1024], P('expert', None, None, 'dp'), may hold values from -0.09375 to 0.09375
- gate_up_scales: bfloat16 [16, 2, 128, 1024], P('expert', None, None, 'dp'), may hold values from 0.5 to 2, as said below
- down_elems: bfloat16 [16, 1024, 4096], P('expert', 'dp'), may hold values from -0.1875 to 0.1875
- down_scales: bfloat16 [16, 32, 4096], P('expert', 'dp'), may hold values from 0.5 to 2, as said below
- swap_pairs: int32 [8], replicated, may hold values 0 or 1
Outputs:
- mixed: bfloat16 [2, 256, 4096], P(None, ('expert', 'dp'))
- new_gate_up_elems: bfloat16 [16, 2, 4096, 1024], P('expert', None, None, 'dp')
- new_gate_up_scales: bfloat16 [16, 2, 128, 1024], P('expert', None, None, 'dp')
- new_down_elems: bfloat16 [16, 1024, 4096], P('expert', 'dp')
- new_down_scales: bfloat16 [16, 32, 4096], P('expert', 'dp')
The draws below stay inside these ranges and needn't reach their ends.
Inputs may be any that keep to these rules, and one draw needn't show every extreme that they name: `route_ids`: within a step each row names 8 different experts; among the 8 rows of one device in a step, at most 8 name any one expert, and exactly 8 do for some expert. `gate_up_scales`: every entry is a power of two. `down_scales`: every entry is a power of two.
All inputs are finite; a program needn't handle non-finite values.
Results may differ from the reference program's by a relative error of at most 0.0077.
Values may be sent and summed in bfloat16 or wider, within the bound.
No kernel may reach another device: no remote copies, remote signals or barrier semaphores. Data moves between devices by JAX's collectives and lax.ppermute only.
A program may use at most 128 MiB of HBM per device.

```python
import math
import jax
import jax.numpy as jnp
import numpy as np
from jax import lax

D = 4096
FF = 1024
TOP = 8
STEPS = 2
ROWS = 8
EXPERTS = 16
FF_DEV = 512
CAP = 8
ROWS_ALL = 256
PAIRS = 8
N_EXPERT = 16
N_DP = 2


def draw_gate_up_scales(key, part):
    powers = jax.random.randint(key, (EXPERTS, 2, D // 32, FF), -1, 2)
    return jnp.exp2(powers.astype(jnp.float32)).astype(jnp.bfloat16)


def draw_down_scales(key, part):
    powers = jax.random.randint(key, (EXPERTS, FF // 32, D), -1, 2)
    return jnp.exp2(powers.astype(jnp.float32)).astype(jnp.bfloat16)


def touch_ends(entries, rng, smallest, high):
    longest = entries.shape.index(max(entries.shape))
    spots = []
    for shift in (0, 1):
        where = [jax.random.randint(jax.random.fold_in(rng, axis), (), 0, length) for axis, length in enumerate(entries.shape)]
        where[longest] = (where[longest] + shift) % entries.shape[longest]
        spots.append(tuple(where))
    return entries.at[spots[0]].set(smallest).at[spots[1]].set(high)


def block_scale(stream_key, shape, split, smallest, high):
    def one(axis_at, parts):
        heights = jax.random.uniform(jax.random.fold_in(jax.random.fold_in(stream_key, 6), axis_at), (parts,), jnp.float32, smallest / len(split), high / len(split))
        return jnp.repeat(jnp.exp(heights), shape[axis_at] // parts).reshape((-1,) + (1,) * (len(shape) - axis_at - 1))

    gain = one(*split[0])
    for cut in split[1:]:
        gain = gain * one(*cut)
    return gain


def routed_block(rng, own, number, rows, number_of, top, limit, slope):
    ranking = jax.random.permutation(rng, number_of)
    heavy_load, usual = portions_of(number_of, rows * top, limit, slope, True), portions_of(number_of, rows * top, limit, slope, False)
    places = jnp.arange(number_of)

    def named(tallies, turn):
        used = int((tallies > 0).sum())
        fixed = max(1, used // 4)
        passed = fixed + (places - fixed + turn * (used - fixed)) % max(1, number_of - fixed)
        return jnp.zeros((number_of,), jnp.int32).at[ranking[jnp.where(places < fixed, places, passed)]].set(jnp.asarray(tallies, jnp.int32))

    tallies = jnp.where(number % 4 == 0, named(heavy_load, number // 4), named(usual, number - number // 4 - 1))
    mixed = jax.random.permutation(jax.random.fold_in(own, 3), number_of)
    giver, receiver = mixed[0:number_of // 2 * 2:2], mixed[1:number_of // 2 * 2:2]
    margin = jnp.minimum(tallies[giver] - 1, limit - tallies[receiver]) // 2
    margin = jnp.where((giver == ranking[0]) | (receiver == ranking[0]) | (tallies[receiver] == 0), 0, jnp.maximum(margin, 0))
    passed = jax.random.randint(jax.random.fold_in(own, 4), (number_of // 2,), 0, 1 << 20) % (margin + 1)
    tallies = tallies.at[giver].add(-passed).at[receiver].add(passed)
    labels = jnp.searchsorted(jnp.cumsum(tallies), jnp.arange(rows * top), side="right").astype(jnp.int32)
    grid = labels.reshape(top, rows).T
    grid = grid[jax.random.permutation(jax.random.fold_in(own, 1), rows)]
    turn = jax.random.randint(jax.random.fold_in(own, 2), (rows, 1), 0, top)
    return jnp.take_along_axis(grid, (jnp.arange(top)[None, :] + turn) % top, axis=1)


def portions_of(count, total, limit, lean, full):
    loads = [(1 << 20) // math.isqrt(rank ** lean) + 1 for rank in range(1, count + 1)]
    largest = limit if full else min(limit, max(-(-total // count), total * loads[0] // sum(loads)))
    least = 1 if total - largest >= count - 1 else 0
    given, spare = [largest] + [least] * (count - 1), total - largest - least * (count - 1)
    while spare > 0:
        candidates = [i for i in range(1, count) if given[i] < largest] or [i for i in range(1, count) if given[i] < limit]
        whole, remaining = sum([loads[i] for i in candidates]), spare
        for i in candidates:
            addition = min(limit - given[i], max(1, remaining * loads[i] // whole), spare)
            given[i] = given[i] + addition
            spare = spare - addition
    return np.array(given)


def gaussian(stream_key, shape, scale, reach, split=(), kind=jnp.bfloat16):
    drawn = scale * jax.random.normal(stream_key, shape, jnp.float32)
    if split:
        drawn = drawn * block_scale(stream_key, shape, split, -0.22, 0.18)
    return jnp.clip(drawn, -reach, reach).astype(kind)


def setup_inputs(seed: int = 0) -> dict:
    splits = jax.random.split(jax.random.key(seed), 11)
    tokens = gaussian(splits[0], (STEPS, ROWS_ALL, D), 1.0, 6.0, ((1, 32),))
    norm_gain = jnp.clip(1.0 + 0.1 * jax.random.normal(splits[1], (D,), jnp.float32), 0.5, 1.5)
    route_ids_keys = jax.random.split(jax.random.fold_in(splits[2], 1), STEPS * ROWS_ALL // ROWS)
    route_ids_turns = jax.random.permutation(jax.random.fold_in(splits[2], 3), STEPS * ROWS_ALL // ROWS)
    route_ids = jax.vmap(lambda own, number: routed_block(jax.random.fold_in(splits[2], 2), own, number, ROWS, EXPERTS, TOP, CAP, 2))(route_ids_keys, route_ids_turns).reshape((STEPS, ROWS_ALL, TOP))
    route_weights = jnp.clip(0.05 + 0.2 * jax.random.uniform(splits[3], (STEPS, ROWS_ALL, TOP), jnp.float32) ** block_scale(splits[3], (STEPS, ROWS_ALL, TOP), ((1, 32),), -0.2, 0.2), 0.05, 0.25)
    rows_left = touch_ends(jax.random.randint(splits[4], (ROWS_ALL,), 1, 20 * STEPS + 1), jax.random.fold_in(splits[4], 1), 1, 20 * STEPS).astype(jnp.int32)
    gate_up_elems = gaussian(splits[5], (EXPERTS, 2, D, FF), D ** -0.5, 0.09375, ((0, 16), (3, 2)))
    gate_up_scales = draw_gate_up_scales(jax.random.fold_in(splits[10], 71), 0)
    down_elems = gaussian(splits[7], (EXPERTS, FF, D), FF ** -0.5, 0.1875, ((0, 16), (1, 2)))
    down_scales = draw_down_scales(jax.random.fold_in(splits[10], 71), 0)
    swap_pairs = touch_ends((jax.random.randint(splits[9], (PAIRS,), 0, 2) < 1).astype(jnp.int32), jax.random.fold_in(splits[9], 1), 0, 1)
    return {"tokens": tokens, "norm_gain": norm_gain, "route_ids": route_ids, "route_weights": route_weights, "rows_left": rows_left, "gate_up_elems": gate_up_elems, "gate_up_scales": gate_up_scales, "down_elems": down_elems, "down_scales": down_scales, "swap_pairs": swap_pairs}


mx_block = 32

def dequantize(elems, scales, axis):
    return elems * jnp.repeat(scales, mx_block, axis=axis)

def rms_normed(rows, norm_gain):
    values = rows.astype(jnp.float32)
    factor = lax.rsqrt(lax.optimization_barrier(jnp.mean(values * values, axis=-1, keepdims=True)) + 1e-06)
    return (values * factor * norm_gain).astype(jnp.bfloat16)

def expert_hidden(rows, gate_up):
    both = jnp.einsum('rd,gdf->grf', rows.astype(jnp.float32), gate_up.astype(jnp.float32))
    return (jax.nn.silu(both[0]) * both[1]).astype(jnp.bfloat16)

def reference(tokens, norm_gain, route_ids, route_weights, rows_left, gate_up_elems, gate_up_scales, down_elems, down_scales, swap_pairs):
    half = EXPERTS // 2
    flags = jnp.concatenate([swap_pairs, swap_pairs])

    def moved(table):
        shape = (table.shape[0],) + (1,) * (table.ndim - 1)
        return jnp.where(flags.reshape(shape) > 0, jnp.roll(table, half, axis=0), table)
    load = CAP * N_EXPERT * N_DP
    count = ROWS_ALL * TOP
    experts_iota = jnp.arange(EXPERTS, dtype=jnp.int32)
    results = []
    for step in range(STEPS):
        normed = rms_normed(tokens[step], norm_gain)
        live = rows_left > step
        flat_live = jnp.repeat(live, TOP)
        target = jnp.where(flat_live, route_ids[step].reshape(-1), EXPERTS).astype(jnp.int32)
        hits = (target[:, None] == experts_iota[None, :]).astype(jnp.int32)
        rank = lax.optimization_barrier(jnp.sum(jnp.cumsum(hits, axis=0) * hits, axis=1)) - 1
        rank = jnp.where(flat_live, rank, load).astype(jnp.int32)
        owners = (jnp.arange(count, dtype=jnp.int32) // TOP).astype(jnp.int32)
        table = jnp.full((EXPERTS, load), ROWS_ALL, jnp.int32).at[target, rank].set(owners, mode='drop')
        padded = jnp.concatenate([normed, jnp.zeros((1, D), jnp.bfloat16)], axis=0)

        def one_expert(index):
            rows_e = padded[table[index]]
            gate_up = dequantize(gate_up_elems[index], gate_up_scales[index], 1)
            down = dequantize(down_elems[index], down_scales[index], 0)
            hidden = expert_hidden(rows_e, gate_up)
            total = jnp.zeros((load, D), jnp.float32)
            for block in range(N_DP):
                part = jnp.dot(hidden[:, block * FF_DEV:(block + 1) * FF_DEV], down[block * FF_DEV:(block + 1) * FF_DEV], preferred_element_type=jnp.float32)
                total = total + lax.optimization_barrier(part.astype(jnp.bfloat16)).astype(jnp.float32)
            return total.astype(jnp.bfloat16)
        outputs = lax.map(one_expert, experts_iota)
        picked = outputs[jnp.minimum(target, EXPERTS - 1), jnp.clip(rank, 0, load - 1)]
        factor = route_weights[step].reshape(-1) * flat_live.astype(jnp.float32)
        mixed_step = lax.optimization_barrier(jnp.sum((picked.astype(jnp.float32) * factor[:, None]).reshape(ROWS_ALL, TOP, D), axis=1))
        results.append(mixed_step.astype(jnp.bfloat16))
    mixed = jnp.stack(results)
    return (mixed, moved(gate_up_elems), moved(gate_up_scales), moved(down_elems), moved(down_scales))
```

```python
import jax
import jax.numpy as jnp
from jax import lax
from jax.experimental import pallas as pl
from jax.experimental.pallas import tpu as pltpu
from jax.sharding import PartitionSpec as P


mx_block = 32
columns = 4


def flip(x, axis, bit):
    return lax.ppermute(x, axis, [(i, i ^ 1 << bit) for i in range(lax.axis_size(axis))])


def dequantize(elems, scales, axis):
    return elems * jnp.repeat(scales, mx_block, axis=axis)


def rms_normed(rows, norm_gain):
    values = rows.astype(jnp.float32)
    factor = lax.rsqrt(jnp.mean(values * values, axis=-1, keepdims=True) + 1e-06)
    return (values * factor * norm_gain).astype(jnp.bfloat16)


def expert_hidden(rows, gate_up):
    both = jnp.einsum("rd,gdf->grf", rows, gate_up, preferred_element_type=jnp.float32)
    return (jax.nn.silu(both[0]) * both[1]).astype(jnp.bfloat16)


def hops(x, axis, low, radix, pick=lambda x, d: x):
    n = lax.axis_size(axis)
    got = []
    for d in range(1, radix):
        got.append(lax.ppermute(pick(x, d), axis, [(i, i ^ d << low) for i in range(n)]))
    return got


def stages():
    bits = lax.axis_size("expert").bit_length() - 1
    order = [("expert", b - 2, 4) for b in range(bits, 1, -2)]
    if bits % 2:
        order = [("expert", 0, 2)] + [("expert", b - 2, 4) for b in range(bits, 2, -2)]
    low = 0
    size = lax.axis_size("dp")
    while size > 1:
        order.append(("dp", low, 2))
        low, size = low + 1, size // 2
    return order


def after(x, *others):
    return lax.optimization_barrier((x, *others))


def total(xs):
    out = xs[0].astype(jnp.float32)
    for x in xs[1:]:
        out = out + x.astype(jnp.float32)
    return out.astype(jnp.bfloat16)


def sender(tokens, norm_gain, route_ids, route_weights, rows_left):
    steps, rows, width = tokens.shape
    slots = lax.axis_size("expert")
    normed = rms_normed(tokens, norm_gain).reshape(steps * rows, width)
    live = (rows_left[None, :] > jnp.arange(steps)[:, None]).astype(jnp.float32)
    hits = route_ids[..., None] == jnp.arange(slots, dtype=jnp.int32)
    share = jnp.sum(jnp.where(hits, (route_weights * live[..., None])[..., None], 0.0), axis=2)
    share = share.reshape(steps * rows, slots)
    parts = []
    for _ in range(3):
        part = lax.reduce_precision(share, 8, 7)
        parts.append(part.astype(jnp.bfloat16))
        share = share - part
    parts = jnp.concatenate(parts, axis=1)
    parts = jnp.pad(parts, ((0, 0), (0, -parts.shape[1] % 128)))
    return jnp.concatenate([parts, normed], axis=1), parts.shape[1]


def expert_rows(everything, side, weights):
    gate_up_elems, gate_up_scales, down_elems, down_scales = weights
    slots = lax.axis_size("expert")
    here = lax.axis_index("expert")
    column = jnp.arange(side, dtype=jnp.int32)
    mine = (column % slots == here) & (column < 3 * slots)
    factor = jnp.sum(
        jnp.where(mine, everything[:, :side].astype(jnp.float32), 0.0), axis=1, keepdims=True
    )
    hidden = expert_hidden(
        everything[:, side:], dequantize(gate_up_elems[0], gate_up_scales[0], 1)
    )
    out = jnp.dot(
        hidden, dequantize(down_elems[0], down_scales[0], 0), preferred_element_type=jnp.float32
    )
    return (out * factor).astype(jnp.bfloat16)


def gather_stage(block, stage):
    return jnp.concatenate([block, *hops(block, *stage)])


def scatter_stage(block, stage):
    n = block.shape[0] // stage[2]
    others = hops(block, *stage, pick=lambda x, d: x[d * n : (d + 1) * n])
    return total([block[:n], *others])


eighths = (0, 1, 3, 4, 5, 6, 8)


def row_map(down_shape, down_s_rows, gate_up_s_rows, gate_up_rows, hidden):
    rows, width = down_shape
    blocks = width // hidden
    first = blocks * 5 // 8
    entries = [(0, b * rows, 2, 0, b * hidden, rows) for b in range(first)]
    runs = [(2, 0, b * hidden, rows) for b in range(first, blocks)]
    runs += [(3, 0, b * hidden, down_s_rows) for b in range(blocks)]
    runs += [(1, 0, 0, gate_up_s_rows), (0, 0, 0, gate_up_rows)]
    length = sum(run[3] for run in runs)
    cuts = [length * e // 64 * 8 for e in eighths]
    cuts[-1] = length
    at = 0
    for array, row, column, count in runs:
        while count:
            k = max(j for j in range(len(cuts) - 1) if cuts[j] <= at)
            size = min(count, cuts[k + 1] - at)
            entries.append((k + 1, at - cuts[k], array, row, column, size))
            at, row, count = at + size, row + size, count - size
    heights = [first * rows] + [b - a for a, b in zip(cuts, cuts[1:])]
    return heights, entries


def copies(moves, buffer, in_sems, out_sems):
    at, arriving, leaving = 0, [], []
    for k, (src, dst) in enumerate(moves):
        rows = buffer.at[pl.ds(at, src.shape[0]), :]
        at += src.shape[0]
        arriving.append(pltpu.make_async_copy(src, rows, in_sems.at[k]))
        leaving.append(pltpu.make_async_copy(rows, dst, out_sems.at[k]))
    for copy in arriving:
        copy.start()
    for into, out in zip(arriving, leaving):
        into.wait()
        out.start()
    for copy in leaving:
        copy.wait()


def staging(entries, hidden):
    return [
        pltpu.VMEM((sum(entry[-1] for entry in entries), hidden), jnp.bfloat16),
        pltpu.SemaphoreType.DMA((len(entries),)),
        pltpu.SemaphoreType.DMA((len(entries),)),
    ]


def gather_blocks(arrays, heights, entries, hidden):
    def body(*refs):
        ins, outs, scratch = refs[:4], refs[4:-3], refs[-3:]
        copies(
            [
                (
                    ins[a].at[pl.ds(row, n), pl.ds(column, hidden)],
                    outs[block].at[pl.ds(at, n), :],
                )
                for block, at, a, row, column, n in entries
            ],
            *scratch,
        )

    hbm = pl.BlockSpec(memory_space=pl.ANY)
    return pl.pallas_call(
        body,
        out_shape=[jax.ShapeDtypeStruct((h, hidden), jnp.bfloat16) for h in heights],
        in_specs=[hbm] * 4,
        out_specs=[hbm] * len(heights),
        scratch_shapes=staging(entries, hidden),
        name="gather_blocks",
    )(*arrays)


def place_blocks(choice, arrays, early, received, entries, hidden):
    planes, count = len(received), len(received[0])

    def body(choice_ref, *refs):
        own, first, refs = refs[:4], refs[4], refs[5:]
        segments = [refs[p * count : (p + 1) * count] for p in range(planes)]
        outs, scratch = refs[planes * count : -3], refs[-3:]

        def rectangle(arrays, entry):
            _, _, a, row, column, n = entry
            return arrays[a].at[pl.ds(row, n), pl.ds(column, hidden)]

        @pl.when(choice_ref[0] == 0)
        def _():
            copies([(rectangle(own, e), rectangle(outs, e)) for e in entries], *scratch)

        for p in range(planes):

            @pl.when(choice_ref[0] == p + 1)
            def _():
                blocks = [first, *segments[p]]
                copies(
                    [(blocks[e[0]].at[pl.ds(e[1], e[-1]), :], rectangle(outs, e)) for e in entries],
                    *scratch,
                )

    hbm = pl.BlockSpec(memory_space=pl.ANY)
    flat = [x for got in received for x in got]
    return pl.pallas_call(
        body,
        out_shape=[jax.ShapeDtypeStruct(x.shape, x.dtype) for x in arrays],
        in_specs=[pl.BlockSpec(memory_space=pltpu.SMEM)] + [hbm] * (5 + len(flat)),
        out_specs=[hbm] * 4,
        scratch_shapes=staging(entries, hidden),
        name="place_blocks",
    )(choice, *arrays, early, *flat)


def moved_pairs(mask, plane, half, own, held):
    active = [c for c in range(columns) if mask >> c & 1]
    if not active:
        return tuple(jnp.zeros_like(x) for x in own)

    def send(x, pairs):
        pairs = [
            (s * half + plane * columns + a, (1 - s) * half + plane * columns + b)
            for a, b in pairs
            for s in (0, 1)
        ]
        return lax.ppermute(x, "expert", pairs)

    direct = [(c, c) for c in active]
    if len(active) == 4:
        return tuple(send(x, direct) for x in own)
    if len(active) == 1:
        c = active[0]
        x = [send(held[k], [(c ^ 1, c)]) for k in (0, 1)]
        y = [send(held[k], [(c ^ 2, c)]) for k in (4, 5)]
        return (*x, send(own[2], direct), send(own[3], direct), *y)
    if len(active) == 2:
        a, b = active
        d = 2 if a ^ b == 1 else 1
        helped = (3, 4, 5) if d == 2 else (0, 1, 2)
        return tuple(
            send(held[k], [(a ^ d, a), (b ^ d, b)]) if k in helped else send(own[k], direct)
            for k in range(6)
        )
    h = (set(range(columns)) - set(active)).pop()
    a, b, d = h ^ 1, h ^ 2, h ^ 3
    me = lax.axis_index("expert") % columns
    front = [
        send(jnp.where(me == h, held[k], own[k]), [(h, a), (b, b), (d, d)]) for k in (0, 1, 2)
    ]
    back = send(held[5], [(h, b), (a, d)])
    own_back = send(own[5], [(a, a)])
    return (*front, send(own[3], direct), send(own[4], direct), jnp.where(me == a, own_back, back))


def on_device(
    tokens,
    norm_gain,
    route_ids,
    route_weights,
    rows_left,
    gate_up_elems,
    gate_up_scales,
    down_elems,
    down_scales,
    swap_pairs,
):
    weights = (gate_up_elems, gate_up_scales, down_elems, down_scales)
    slots = lax.axis_size("expert")
    half = slots // 2
    top_bit = slots.bit_length() - 2
    pair = lax.axis_index("expert") % half
    flag = jnp.sum(jnp.where(jnp.arange(half, dtype=jnp.int32) == pair, swap_pairs, 0)) > 0
    block, side = sender(tokens, norm_gain, route_ids, route_weights, rows_left)
    order = stages()
    planes = half // columns
    if planes != 2:
        received = flip(weights, "expert", top_bit)
        for stage in order:
            block = gather_stage(block, stage)
        block = expert_rows(block, side, weights)
        for stage in reversed(order):
            block = scatter_stage(block, stage)
        new = tuple((jnp.where(flag, other, mine) for mine, other in zip(weights, received)))
        return (block.reshape(tokens.shape), *new)

    hidden = gate_up_elems.shape[3]
    flat = (
        gate_up_elems.reshape(-1, hidden),
        gate_up_scales.reshape(-1, hidden),
        down_elems[0],
        down_scales[0],
    )
    heights, entries = row_map(
        flat[2].shape, flat[3].shape[0], flat[1].shape[0], flat[0].shape[0], hidden
    )
    early, *own = gather_blocks(flat, heights, entries, hidden)
    held = [None] * 6

    def spread(ks, *tied):
        tied, given = tied[0], [own[k] for k in ks]
        if tied is not None:
            tied, *given = after(tied, *given)
        for k, x in zip(ks, given):
            held[k] = flip(x, "expert", 0 if k < 3 else 1)
        return tied

    z_stage, plane_stage, dp_stages = order[0], order[1], order[2:]
    spread((0, 3), None)
    block = gather_stage(block, z_stage)
    block, early = after(block, early)
    early = flip(early, "expert", top_bit)
    block = gather_stage(block, plane_stage)
    block = spread((1, 5), block)
    for stage in dp_stages:
        block = gather_stage(block, stage)
    block = expert_rows(block, side, weights)
    for stage in reversed(dp_stages):
        block = scatter_stage(block, stage)
    block = scatter_stage(block, plane_stage)
    block = spread((2, 4), block)
    block = scatter_stage(block, z_stage)
    mixed, swap_pairs, early, *held = after(block, swap_pairs, early, *held)
    received = []
    for plane in range(planes):
        bits = swap_pairs[plane * columns : (plane + 1) * columns]
        mask = jnp.sum(jnp.where(bits > 0, 1 << jnp.arange(columns, dtype=jnp.int32), 0))
        got = lax.switch(
            mask,
            [
                (lambda m: lambda own, held: moved_pairs(m, plane, half, own, held))(m)
                for m in range(1 << columns)
            ],
            tuple(own),
            tuple(held),
        )
        received.append(got)
    choice = jnp.where(flag, 1 + pair // columns, 0).astype(jnp.int32).reshape(1)
    new = place_blocks(choice, flat, early, received, entries, hidden)
    return (
        mixed.reshape(tokens.shape),
        *(x.reshape(old.shape) for x, old in zip(new, weights)),
    )


def solution(mesh):
    in_specs = (
        P(None, ("expert", "dp"), None),
        P(),
        P(None, ("expert", "dp"), None),
        P(None, ("expert", "dp"), None),
        P(("expert", "dp")),
        P("expert", None, None, "dp"),
        P("expert", None, None, "dp"),
        P("expert", "dp", None),
        P("expert", "dp", None),
        P(),
    )
    out_specs = (
        P(None, ("expert", "dp"), None),
        P("expert", None, None, "dp"),
        P("expert", None, None, "dp"),
        P("expert", "dp", None),
        P("expert", "dp", None),
    )

    return jax.shard_map(
        on_device, mesh=mesh, in_specs=in_specs, out_specs=out_specs, check_vma=False
    )
```
